32 devices in a mesh: leaf: 32 (over z, y, x, core).
Axes of the slice: x: 2, y: 2, z: 4, core: 2. Of those that a mesh axis runs over, the one named last changes fastest.
Arguments:
- points: bfloat16 [64, 32768], P(None, 'leaf'), may hold values from -6 to 6
- weights: bfloat16 [32768, 512], P('leaf'), may hold values from -1.1953125 to 1.1953125
- interp: bfloat16 [32768, 512], P('leaf'), may hold values from -0.1875 to 0.1875
- transfers: bfloat16 [32, 5, 512, 512], P('leaf'), may hold values from -0.25 to 0.25
- near_mask: int32 [32, 4], P('leaf'), may hold values 0 or 1
- skel_index: int32 [32, 512], P('leaf'), may hold values from 0 to 1023, as said below
Outputs:
- product: bfloat16 [32768, 512], P('leaf')
The draws below stay inside these ranges and needn't reach their ends.
Inputs may be any that keep to these rules, and one draw needn't show every extreme that they name: `skel_index`: each row holds 512 distinct ranks.
All inputs are finite; a program needn't handle non-finite values. No bound on the sum of `near_mask` on one device may be relied on, other than what follows from the above.
Results may differ from the reference program's by a relative error of at most 0.0075.
Values may be sent and summed in bfloat16 or wider, within the bound.
A program may use at most 128 MiB of HBM per device.

```python
import jax
import jax.numpy as jnp
from jax import lax

DIM = 64
RHS = 512
S = 512
NPTS = 1024
LEVELS = 5
RADIUS = 2
LEAVES = 32
POINTS = 32768


def pick_row(row_key):
    return jax.random.permutation(row_key, NPTS)[:S]


def draw_skel_index(key, part):
    row_keys = jax.random.split(jax.random.fold_in(key, 17), LEAVES)
    return jax.vmap(pick_row)(row_keys).astype(jnp.int32)


def set_ends(array, stream_key, low, largest):
    index_at = [jax.random.randint(jax.random.fold_in(stream_key, axis), (), 0, length) for axis, length in enumerate(array.shape)]
    widest = array.shape.index(max(array.shape))
    next_to = index_at[:widest] + [(index_at[widest] + 1) % array.shape[widest]] + index_at[widest + 1:]
    return array.at[tuple(index_at)].set(low).at[tuple(next_to)].set(largest)


def levels(stream_key, extent, shards, smallest, top_value):
    def one(axis_at, parts):
        steps = jax.random.uniform(jax.random.fold_in(jax.random.fold_in(stream_key, 6), axis_at), (parts,), jnp.float32, smallest / len(shards), top_value / len(shards))
        return jnp.repeat(jnp.exp(steps), extent[axis_at] // parts).reshape((-1,) + (1,) * (len(extent) - axis_at - 1))

    factor_of = one(*shards[0])
    for cut in shards[1:]:
        factor_of = factor_of * one(*cut)
    return factor_of


def centred(own_key, shape, deviation, most, cuts=(), held_as=jnp.bfloat16):
    gain = levels(own_key, shape, cuts, -0.22, 0.18) if cuts else 1.0
    drawn = jax.random.normal(own_key, shape, jnp.float32) * deviation * gain
    return jnp.minimum(jnp.maximum(drawn, -most), most).astype(held_as)


def setup_inputs(seed: int = 0) -> dict:
    streams_of = jax.random.split(jax.random.key(seed), 7)
    return {
        "points": centred(streams_of[0], (DIM, POINTS), 1.0, 6.0, ((1, 32),)),
        "weights": centred(streams_of[1], (POINTS, RHS), 0.2, 1.1953125, ((0, 32),)),
        "interp": centred(streams_of[2], (POINTS, S), NPTS ** -0.5, 0.1875, ((0, 32),)),
        "transfers": centred(streams_of[3], (LEAVES, LEVELS, S, S), S ** -0.5, 0.25, ((0, 32),)),
        "near_mask": set_ends((jax.random.randint(streams_of[4], (LEAVES, 2 * RADIUS), 0, 4) < 3).astype(jnp.int32), jax.random.fold_in(streams_of[4], 1), 0, 1),
        "skel_index": draw_skel_index(jax.random.fold_in(streams_of[6], 71), 0),
    }


def widened(value):
    return lax.optimization_barrier(value).astype(jnp.float32)


def kernel_tile(left, right):
    left_wide = left.astype(jnp.float32)
    right_wide = right.astype(jnp.float32)
    sq_left = jnp.sum(left_wide * left_wide, axis=0)
    sq_right = jnp.sum(right_wide * right_wide, axis=0)
    cross_terms = lax.dot_general(left, right, (((0,), (0,)), ((), ())), preferred_element_type=jnp.float32)
    distance = sq_left[:, None] + sq_right[None, :] - 2.0 * cross_terms
    return jnp.exp(distance * (-1.0 / DIM)).astype(jnp.bfloat16)


def reference(points, weights, interp, transfers, near_mask, skel_index):
    leaf_points = points.reshape(DIM, LEAVES, NPTS).transpose(1, 0, 2)
    leaf_weights_in = weights.reshape(LEAVES, NPTS, RHS)
    leaf_interp = interp.reshape(LEAVES, NPTS, S)
    offsets = list(range(-RADIUS, 0)) + list(range(1, RADIUS + 1))

    def near_leaf(leaf_id):
        own_points = leaf_points[leaf_id]
        total = jnp.dot(kernel_tile(own_points, own_points), leaf_weights_in[leaf_id], preferred_element_type=jnp.float32)
        for slot_index, offset in enumerate(offsets):
            target = leaf_id + offset
            neighbour = jnp.clip(target, 0, LEAVES - 1)
            in_range = (target >= 0) & (target < LEAVES)
            flag_value = jnp.where(in_range, near_mask[leaf_id, slot_index], 0).astype(jnp.float32)
            block = jnp.dot(kernel_tile(own_points, leaf_points[neighbour]), leaf_weights_in[neighbour], preferred_element_type=jnp.float32)
            total = total + flag_value * block
        return total

    leaf_ids = jnp.arange(LEAVES, dtype=jnp.int32)
    near_field = lax.map(near_leaf, leaf_ids)
    skel_points = jnp.take_along_axis(leaf_points, skel_index[:, None, :], axis=2)
    leaf_weights = jnp.einsum("nps,npr->nsr", widened(leaf_interp), widened(leaf_weights_in)).astype(jnp.bfloat16)
    far_sum = jnp.zeros((LEAVES, S, RHS), jnp.float32)
    for level in range(LEVELS):
        transfer_level = widened(transfers[:, level])
        level_terms = jnp.einsum("nab,nar->nbr", transfer_level, widened(leaf_weights))
        nodes = LEAVES >> level
        group = 2 ** level
        node_sums = level_terms.reshape(nodes, group, S, RHS).sum(axis=1).astype(jnp.bfloat16)
        columns_kept = S >> level
        node_points = skel_points[:, :, :columns_kept].reshape(nodes, group, DIM, columns_kept)
        node_points = node_points.transpose(0, 2, 1, 3).reshape(nodes, DIM, S)

        def couple_node(node_id):
            partner = node_id ^ 1
            tile = kernel_tile(node_points[node_id], node_points[partner])
            return jnp.dot(tile, node_sums[partner], preferred_element_type=jnp.float32).astype(jnp.bfloat16)

        coupled = lax.map(couple_node, jnp.arange(nodes, dtype=jnp.int32))
        coupled_leaf = jnp.repeat(coupled, group, axis=0)
        far_sum = far_sum + jnp.einsum("nab,nbr->nar", transfer_level, widened(coupled_leaf))
    far_skeleton = far_sum.astype(jnp.bfloat16)
    far_field = jnp.einsum("nps,nsr->npr", widened(leaf_interp), widened(far_skeleton))
    return (near_field + far_field).astype(jnp.bfloat16).reshape(POINTS, RHS)
```

```python
import functools
import math

import jax
import jax.numpy as jnp
from jax import lax
from jax.experimental import pallas as pl
from jax.experimental.pallas import tpu as pltpu
from jax.sharding import PartitionSpec as P

MESH = pl.DeviceIdType.MESH
LANES = 128
CHUNKS = 4
F32, BF16 = jnp.float32, jnp.bfloat16


def rounded(value):
    return value.astype(BF16).astype(F32)


def dot(left, right, dims=((1,), (0,))):
    return lax.dot_general(left, right, (dims, ((), ())), preferred_element_type=F32)


def left_form(wide, dim):
    lane = lax.broadcasted_iota(jnp.int32, wide.shape, 1)
    norm = jnp.sum(jnp.where((lane >= dim) & (lane < dim + 3), wide, 0.0), axis=1, keepdims=True)
    left = jnp.where(lane < dim, 2.0 * wide, jnp.where(lane < dim + 3, -1.0, 0.0))
    return left.astype(BF16), norm


def reduce_bits(level):
    return [0] + list(range(level - 1, 0, -1)) if level else []


def plan(levels):
    names = []
    for level in range(levels):
        for bit in reduce_bits(level):
            names += [("rs", level, bit), ("ag", level, bit)]
        names += [("ex", level), ("pt", level)]
    for chunk in range(CHUNKS + 1):
        names += [("own_mate", chunk), ("own_x", chunk), ("fwd", chunk), ("fwd_mate", chunk)]
    return {name: at for at, name in enumerate(names)}


def body(
    count, slots,
    pts, w, interp, trans, mask, index,
    out,
    rown, lown, nown, rbuf, wbuf, near, lw, keep, tx, rx, sib, pbuf, psib, far,
    send_sem, recv_sem,
):
    me = lax.axis_index("leaf")
    core, chip = lax.rem(me, 2), lax.rem(me // 2, 2)
    dim, npts = pts.shape
    rank, rhs = lw.shape
    levels = trans.shape[0]
    deep = rown.shape[0]
    scale = math.log2(math.e) / dim

    def partner(bit):
        on = lax.rem(me // (1 << bit), 2)
        return me + (1 - 2 * on) * (1 << bit), on

    mate, xmate = partner(0)[0], partner(1)[0]
    ahead = me + 4 * (1 - 2 * chip)
    behind = me - 4 * (1 - 2 * chip)
    has_ahead = (ahead >= 0) & (ahead < count)
    has_behind = (behind >= 0) & (behind < count)

    def copy(name, src, dst, device):
        at = slots[name]
        return pltpu.make_async_remote_copy(
            src_ref=src, dst_ref=dst, send_sem=send_sem.at[at], recv_sem=recv_sem.at[at],
            device_id=(device,), device_id_type=MESH,
        )

    barrier = pltpu.get_barrier_semaphore()
    for bit in range(levels):
        pl.semaphore_signal(barrier, inc=1, device_id=(partner(bit)[0],), device_id_type=MESH)
    for other, there in ((ahead, has_ahead), (behind, has_behind)):
        @pl.when(there)
        def _():
            pl.semaphore_signal(barrier, inc=1, device_id=(other,), device_id_type=MESH)

    wide = pts[...].astype(F32)
    norm = jnp.sum(wide * wide, axis=0, keepdims=True)
    high = rounded(norm)
    middle = rounded(norm - high)
    low = norm - high - middle
    row = lax.broadcasted_iota(jnp.int32, (LANES - dim, npts), 0)
    extra = jnp.where(row == 0, high, jnp.where(row == 1, middle, jnp.where(row == 2, low, 0.0)))
    full = jnp.concatenate([wide, extra], axis=0)
    rown[...] = full[:deep].astype(BF16)
    left, norm_column = left_form(jnp.transpose(full), dim)
    lown[...] = left
    nown[...] = norm_column
    chosen = (lax.broadcasted_iota(jnp.int32, (npts, rank), 0) == index[...]).astype(BF16)
    pbuf[0] = jnp.transpose(dot(full.astype(BF16), chosen)).astype(BF16)

    pl.semaphore_wait(barrier, levels + has_ahead.astype(jnp.int32) + has_behind.astype(jnp.int32))

    step = npts // CHUNKS

    def part(chunk):
        return pl.ds((chunk - 1) * step, step)

    def own(kind, chunk, slot, device):
        if chunk == 0:
            return copy((kind, 0), rown, rbuf.at[slot], device)
        return copy((kind, chunk), w.at[part(chunk)], wbuf.at[slot, part(chunk)], device)

    def pass_on(kind, chunk, source, slot, device):
        if chunk == 0:
            return copy((kind, 0), rbuf.at[source], rbuf.at[slot], device)
        return copy((kind, chunk), wbuf.at[source, part(chunk)], wbuf.at[slot, part(chunk)], device)

    def points_copy(level):
        return copy(("pt", level), pbuf.at[level], psib.at[level], partner(level)[0])

    def points_next(level):
        points_copy(level).wait()
        if level + 1 == levels:
            return
        group, width = 1 << level, rank >> level

        def halved(ref):
            return ref[level].reshape(group, width, LANES)[:, : width // 2].reshape(rank // 2, LANES)

        mine, theirs = halved(pbuf), halved(psib)
        upper = partner(level)[1] == 1
        pbuf[level + 1, : rank // 2] = jnp.where(upper, theirs, mine)
        pbuf[level + 1, rank // 2 :] = jnp.where(upper, mine, theirs)
        points_copy(level + 1).start()

    points_copy(0).start()
    for chunk in range(3):
        own("own_x", chunk, 0, xmate).start()

    lw[...] = dot(interp[...], w[...], ((0,), (0,))).astype(BF16)
    half = rank // 2
    kept_at = pl.multiple_of(core * half, half)
    sent_at = pl.multiple_of((1 - core) * half, half)

    def geometry(level, upto):
        bits = reduce_bits(level)
        offset, length = 0, rank
        for bit in bits[:upto]:
            length //= 2
            offset = offset + partner(bit)[1] * length
        if upto:
            offset = pl.multiple_of(offset, length)
        return offset, length

    def reduce_copy(level, at):
        bit = reduce_bits(level)[at]
        length = rank >> (at + 1)
        rows = pl.ds(rank - 2 * length, length)
        return copy(("rs", level, bit), tx.at[level, rows], rx.at[level, rows], partner(bit)[0])

    def exchange_copy(level):
        offset, length = geometry(level, level)
        rows = pl.ds(0 if level == 0 else rank - length, length)
        return copy(("ex", level), tx.at[level, rows], sib.at[level, pl.ds(offset, length)], partner(level)[0])

    def gather_copy(level, at):
        bit = reduce_bits(level)[at]
        offset, length = geometry(level, at + 1)
        rows = pl.ds(offset, length)
        return copy(("ag", level, bit), sib.at[level, rows], sib.at[level, rows], partner(bit)[0])

    for level in range(1, levels):
        tx[level, :half] = dot(trans[level, :, pl.ds(sent_at, half)], lw[...], ((0,), (0,))).astype(BF16)
        reduce_copy(level, 0).start()
        keep[level] = dot(trans[level, :, pl.ds(kept_at, half)], lw[...], ((0,), (0,)))
    tx[0] = dot(trans[0], lw[...], ((0,), (0,))).astype(BF16)
    exchange_copy(0).start()
    for chunk in range(CHUNKS + 1):
        own("own_mate", chunk, 2, mate).start()
    for chunk in range(3, CHUNKS + 1):
        own("own_x", chunk, 0, xmate).start()

    def chain(level):
        bits = reduce_bits(level)
        for at, bit in enumerate(bits):
            reduce_copy(level, at).wait()
            length = rank >> (at + 1)
            total = keep[level, :length] + rx[level, pl.ds(rank - 2 * length, length)].astype(F32)
            if at + 1 < len(bits):
                shorter = length // 2
                upper = partner(bits[at + 1])[1] == 1
                first, second = total[:shorter], total[shorter:]
                tx[level, pl.ds(rank - length, shorter)] = jnp.where(upper, first, second).astype(BF16)
                reduce_copy(level, at + 1).start()
                keep[level, :shorter] = jnp.where(upper, second, first)
            else:
                tx[level, pl.ds(rank - length, length)] = total.astype(BF16)
                exchange_copy(level).start()
            yield
        exchange_copy(level).wait()
        for at in range(len(bits) - 1, -1, -1):
            gather_copy(level, at).start()
            yield
            gather_copy(level, at).wait()

    chains = [chain(level) for level in range(levels)]

    def advance(*which):
        for level in which:
            next(chains[level], None)

    even = chip == 0
    flags = [
        jnp.where(even, mask[0, 3], mask[0, 0]),
        jnp.where(even, mask[0, 0], mask[0, 3]),
        jnp.where(core == 0, mask[0, 2], mask[0, 1]),
        jnp.where(core == 0, mask[0, 1], mask[0, 2]),
    ]
    block = 256

    def near_part(right, weights, flag):
        @pl.loop(0, npts // block)
        def _(at):
            rows = pl.ds(pl.multiple_of(at * block, block), block)
            power = dot(lown[rows, :deep], right[...]) - nown[rows]
            tile = jnp.exp2(power * scale).astype(BF16)
            value = dot(tile, weights[...])
            near[rows] = value if flag is None else near[rows] + flag.astype(F32) * value

    def near_slot(slot):
        near_part(rbuf.at[slot], wbuf.at[slot], flags[slot])

    def couple(level):
        left, norm_own = left_form(pbuf[level].astype(F32), dim)
        power = dot(left, psib[level], ((1,), (1,))) - norm_own
        tile = jnp.exp2(power * scale).astype(BF16)
        coupled = dot(tile, sib[level]).astype(BF16)
        term = dot(trans[level], coupled)
        far[...] = term if level == 0 else far[...] + term

    direct = core == chip

    def relay(chunks):
        for chunk in chunks:
            own("own_x", chunk, 0, xmate).wait_recv()

            @pl.when(has_ahead)
            def _():
                pass_on("fwd", chunk, 0, 1, ahead).start()

            @pl.when(direct)
            def _():
                pass_on("fwd_mate", chunk, 0, 3, mate).start()

    near_part(rown, w, None)
    points_next(0)
    advance(1, 2, 3, 4)
    relay(range(2))
    for chunk in range(CHUNKS + 1):
        own("own_mate", chunk, 2, mate).wait_recv()
    near_slot(2)
    points_next(1)
    advance(1, 2, 3, 4)
    relay(range(2, 3))
    advance(0)
    couple(0)
    points_next(2)
    advance(2, 3, 4, 1)
    relay(range(3, 4))
    couple(1)
    points_next(3)
    advance(2, 3, 4)
    relay(range(4, CHUNKS + 1))
    near_slot(0)
    advance(4, 3, 2)
    points_next(4)
    couple(2)
    advance(4, 3)
    for chunk in range(CHUNKS + 1):
        @pl.when(has_behind)
        def _():
            pass_on("fwd", chunk, 0, 1, ahead).wait_recv()

            @pl.when(jnp.logical_not(direct))
            def _():
                pass_on("fwd_mate", chunk, 1, 3, mate).start()

    advance(4, 3)

    @pl.when(has_behind)
    def _():
        near_slot(1)

    for _ in range(9):
        advance(4, 3)
    couple(3)
    couple(4)

    @pl.when(has_behind | jnp.logical_not(direct))
    def _():
        for chunk in range(CHUNKS + 1):
            pass_on("fwd_mate", chunk, 0, 3, mate).wait_recv()
        near_slot(3)

    total = far[...].astype(BF16)

    @pl.loop(0, npts // block)
    def _(at):
        rows = pl.ds(pl.multiple_of(at * block, block), block)
        out[rows] = (near[rows] + dot(interp[rows], total)).astype(out.dtype)

    for chunk in range(CHUNKS + 1):
        own("own_mate", chunk, 2, mate).wait_send()
        own("own_x", chunk, 0, xmate).wait_send()

        @pl.when(has_ahead)
        def _():
            pass_on("fwd", chunk, 0, 1, ahead).wait_send()

        @pl.when(has_behind | direct)
        def _():
            pass_on("fwd_mate", chunk, 0, 3, mate).wait_send()


def per_device(points, weights, interp, transfers, near_mask, skel_index):
    count = lax.axis_size("leaf")
    dim, npts = points.shape
    rhs, rank = weights.shape[1], interp.shape[1]
    levels = transfers.shape[1]
    deep = -(-(dim + 3) // 16) * 16
    slots = plan(levels)
    vmem = pl.BlockSpec(memory_space=pltpu.VMEM)
    return pl.pallas_call(
        functools.partial(body, count, slots),
        out_shape=jax.ShapeDtypeStruct((npts, rhs), BF16),
        in_specs=[vmem] * 4 + [pl.BlockSpec(memory_space=pltpu.SMEM), vmem],
        out_specs=vmem,
        scratch_shapes=[
            pltpu.VMEM((deep, npts), BF16),
            pltpu.VMEM((npts, LANES), BF16),
            pltpu.VMEM((npts, 1), F32),
            pltpu.VMEM((4, deep, npts), BF16),
            pltpu.VMEM((4, npts, rhs), BF16),
            pltpu.VMEM((npts, rhs), F32),
            pltpu.VMEM((rank, rhs), BF16),
            pltpu.VMEM((levels, rank // 2, rhs), F32),
            pltpu.VMEM((levels, rank, rhs), BF16),
            pltpu.VMEM((levels, rank, rhs), BF16),
            pltpu.VMEM((levels, rank, rhs), BF16),
            pltpu.VMEM((levels, rank, LANES), BF16),
            pltpu.VMEM((levels, rank, LANES), BF16),
            pltpu.VMEM((rank, rhs), F32),
            pltpu.SemaphoreType.DMA((len(slots),)),
            pltpu.SemaphoreType.DMA((len(slots),)),
        ],
        compiler_params=pltpu.CompilerParams(
            collective_id=0, has_side_effects=True, vmem_limit_bytes=60 * 2**20
        ),
    )(points, weights, interp, transfers[0], near_mask, skel_index)


def solution(mesh):
    return jax.shard_map(
        per_device,
        mesh=mesh,
        in_specs=(
            P(None, "leaf"),
            P("leaf", None),
            P("leaf", None),
            P("leaf", None, None, None),
            P("leaf", None),
            P("leaf", None),
        ),
        out_specs=P("leaf", None),
        check_vma=False,
    )
```

```python
import functools
import math

import jax
import jax.numpy as jnp
from jax import lax
from jax.experimental import pallas as pl
from jax.experimental.pallas import tpu as pltpu
from jax.sharding import PartitionSpec as P

MESH = pl.DeviceIdType.MESH
LANES = 128
CHUNKS = 8
F32, BF16 = jnp.float32, jnp.bfloat16


def rounded(value):
    return value.astype(BF16).astype(F32)


def dot(left, right, dims=((1,), (0,))):
    return lax.dot_general(left, right, (dims, ((), ())), preferred_element_type=F32)


def left_form(wide, dim):
    lane = lax.broadcasted_iota(jnp.int32, wide.shape, 1)
    norm = jnp.sum(jnp.where((lane >= dim) & (lane < dim + 3), wide, 0.0), axis=1, keepdims=True)
    left = jnp.where(lane < dim, 2.0 * wide, jnp.where(lane < dim + 3, -1.0, 0.0))
    return left.astype(BF16), norm


def reduce_bits(level):
    return [0] + list(range(level - 1, 0, -1)) if level else []


def plan(levels):
    names = []
    for level in range(levels):
        for bit in reduce_bits(level):
            names += [("rs", level, bit), ("ag", level, bit)]
        names += [("ex", level), ("pt", level)]
    for chunk in range(CHUNKS + 1):
        names += [("own_mate", chunk), ("own_x", chunk), ("fwd", chunk), ("fwd_mate", chunk)]
    return {name: at for at, name in enumerate(names)}


def body(
    count, slots,
    pts, w, interp, trans, mask, index,
    out,
    rown, lown, nown, rbuf, wbuf, near, lw, keep, tx, rx, sib, pbuf, psib, far,
    send_sem, recv_sem,
):
    me = lax.axis_index("leaf")
    core, chip = lax.rem(me, 2), lax.rem(me // 2, 2)
    dim, npts = pts.shape
    rank, rhs = lw.shape
    levels = trans.shape[0]
    deep = rown.shape[0]
    scale = math.log2(math.e) / dim

    def partner(bit):
        on = lax.rem(me // (1 << bit), 2)
        return me + (1 - 2 * on) * (1 << bit), on

    mate, xmate = partner(0)[0], partner(1)[0]
    ahead = me + 4 * (1 - 2 * chip)
    behind = me - 4 * (1 - 2 * chip)
    has_ahead = (ahead >= 0) & (ahead < count)
    has_behind = (behind >= 0) & (behind < count)

    def copy(name, src, dst, device):
        at = slots[name]
        return pltpu.make_async_remote_copy(
            src_ref=src, dst_ref=dst, send_sem=send_sem.at[at], recv_sem=recv_sem.at[at],
            device_id=(device,), device_id_type=MESH,
        )

    barrier = pltpu.get_barrier_semaphore()
    for bit in range(levels):
        pl.semaphore_signal(barrier, inc=1, device_id=(partner(bit)[0],), device_id_type=MESH)
    for other, there in ((ahead, has_ahead), (behind, has_behind)):
        @pl.when(there)
        def _():
            pl.semaphore_signal(barrier, inc=1, device_id=(other,), device_id_type=MESH)

    wide = pts[...].astype(F32)
    norm = jnp.sum(wide * wide, axis=0, keepdims=True)
    high = rounded(norm)
    middle = rounded(norm - high)
    low = norm - high - middle
    row = lax.broadcasted_iota(jnp.int32, (LANES - dim, npts), 0)
    extra = jnp.where(row == 0, high, jnp.where(row == 1, middle, jnp.where(row == 2, low, 0.0)))
    full = jnp.concatenate([wide, extra], axis=0)
    rown[...] = full[:deep].astype(BF16)
    left, norm_column = left_form(jnp.transpose(full), dim)
    lown[...] = left
    nown[...] = norm_column
    chosen = (lax.broadcasted_iota(jnp.int32, (npts, rank), 0) == index[...]).astype(BF16)
    pbuf[0] = jnp.transpose(dot(full.astype(BF16), chosen)).astype(BF16)

    pl.semaphore_wait(barrier, levels + has_ahead.astype(jnp.int32) + has_behind.astype(jnp.int32))

    step = npts // CHUNKS

    def part(chunk):
        return pl.ds((chunk - 1) * step, step)

    def own(kind, chunk, slot, device):
        if chunk == 0:
            return copy((kind, 0), rown, rbuf.at[slot], device)
        return copy((kind, chunk), w.at[part(chunk)], wbuf.at[slot, part(chunk)], device)

    def pass_on(kind, chunk, source, slot, device):
        if chunk == 0:
            return copy((kind, 0), rbuf.at[source], rbuf.at[slot], device)
        return copy((kind, chunk), wbuf.at[source, part(chunk)], wbuf.at[slot, part(chunk)], device)

    def points_copy(level):
        return copy(("pt", level), pbuf.at[level], psib.at[level], partner(level)[0])

    def points_next(level):
        points_copy(level).wait()
        if level + 1 == levels:
            return
        group, width = 1 << level, rank >> level

        def halved(ref):
            return ref[level].reshape(group, width, LANES)[:, : width // 2].reshape(rank // 2, LANES)

        mine, theirs = halved(pbuf), halved(psib)
        upper = partner(level)[1] == 1
        pbuf[level + 1, : rank // 2] = jnp.where(upper, theirs, mine)
        pbuf[level + 1, rank // 2 :] = jnp.where(upper, mine, theirs)
        points_copy(level + 1).start()

    points_copy(0).start()

    def send_x(*chunks):
        for chunk in chunks:
            own("own_x", chunk, 0, xmate).start()

    send_x(0, 1)

    lw[...] = dot(interp[...], w[...], ((0,), (0,))).astype(BF16)
    points_next(0)
    send_x(2)
    half = rank // 2
    kept_at = pl.multiple_of(core * half, half)
    sent_at = pl.multiple_of((1 - core) * half, half)

    def geometry(level, upto):
        bits = reduce_bits(level)
        offset, length = 0, rank
        for bit in bits[:upto]:
            length //= 2
            offset = offset + partner(bit)[1] * length
        if upto:
            offset = pl.multiple_of(offset, length)
        return offset, length

    def reduce_copy(level, at):
        bit = reduce_bits(level)[at]
        length = rank >> (at + 1)
        rows = pl.ds(rank - 2 * length, length)
        return copy(("rs", level, bit), tx.at[level, rows], rx.at[level, rows], partner(bit)[0])

    def exchange_copy(level):
        offset, length = geometry(level, level)
        rows = pl.ds(0 if level == 0 else rank - length, length)
        return copy(("ex", level), tx.at[level, rows], sib.at[level, pl.ds(offset, length)], partner(level)[0])

    def gather_copy(level, at):
        bit = reduce_bits(level)[at]
        offset, length = geometry(level, at + 1)
        rows = pl.ds(offset, length)
        return copy(("ag", level, bit), sib.at[level, rows], sib.at[level, rows], partner(bit)[0])

    for level in range(levels - 1, 0, -1):
        tx[level, :half] = dot(trans[level, :, pl.ds(sent_at, half)], lw[...], ((0,), (0,))).astype(BF16)
        reduce_copy(level, 0).start()
        keep[level] = dot(trans[level, :, pl.ds(kept_at, half)], lw[...], ((0,), (0,)))
    tx[0] = dot(trans[0], lw[...], ((0,), (0,))).astype(BF16)
    exchange_copy(0).start()
    for chunk in range(CHUNKS + 1):
        own("own_mate", chunk, 2, mate).start()

    def chain(level):
        bits = reduce_bits(level)
        for at, bit in enumerate(bits):
            reduce_copy(level, at).wait()
            length = rank >> (at + 1)
            total = keep[level, :length] + rx[level, pl.ds(rank - 2 * length, length)].astype(F32)
            if at + 1 < len(bits):
                shorter = length // 2
                upper = partner(bits[at + 1])[1] == 1
                first, second = total[:shorter], total[shorter:]
                tx[level, pl.ds(rank - length, shorter)] = jnp.where(upper, first, second).astype(BF16)
                reduce_copy(level, at + 1).start()
                keep[level, :shorter] = jnp.where(upper, second, first)
            else:
                tx[level, pl.ds(rank - length, length)] = total.astype(BF16)
                exchange_copy(level).start()
            yield
        exchange_copy(level).wait()
        for at in range(len(bits) - 1, -1, -1):
            gather_copy(level, at).start()
            yield
            gather_copy(level, at).wait()

    chains = [chain(level) for level in range(levels)]

    def advance(*which):
        for level in which:
            next(chains[level], None)

    even = chip == 0
    flags = [
        jnp.where(even, mask[0, 3], mask[0, 0]),
        jnp.where(even, mask[0, 0], mask[0, 3]),
        jnp.where(core == 0, mask[0, 2], mask[0, 1]),
        jnp.where(core == 0, mask[0, 1], mask[0, 2]),
    ]
    block = 256

    def near_part(right, weights, flag, first=0, last=npts // block):
        @pl.loop(first, last)
        def _(at):
            rows = pl.ds(pl.multiple_of(at * block, block), block)
            power = dot(lown[rows, :deep], right[...]) - nown[rows]
            tile = jnp.exp2(power * scale).astype(BF16)
            value = dot(tile, weights[...])
            near[rows] = value if flag is None else near[rows] + flag.astype(F32) * value

    def near_slot(slot):
        near_part(rbuf.at[slot], wbuf.at[slot], flags[slot])

    def couple(level):
        left, norm_own = left_form(pbuf[level].astype(F32), dim)
        power = dot(left, psib[level], ((1,), (1,))) - norm_own
        tile = jnp.exp2(power * scale).astype(BF16)
        coupled = dot(tile, sib[level]).astype(BF16)
        term = dot(trans[level], coupled)
        far[...] = term if level == 0 else far[...] + term

    direct = core == chip

    def relay(*chunks):
        for chunk in chunks:
            own("own_x", chunk, 0, xmate).wait_recv()

            @pl.when(has_ahead)
            def _():
                pass_on("fwd", chunk, 0, 1, ahead).start()

            @pl.when(direct)
            def _():
                pass_on("fwd_mate", chunk, 0, 3, mate).start()

    def relay_on(*chunks):
        for chunk in chunks:
            @pl.when(has_behind)
            def _():
                pass_on("fwd", chunk, 0, 1, ahead).wait_recv()

                @pl.when(jnp.logical_not(direct))
                def _():
                    pass_on("fwd_mate", chunk, 1, 3, mate).start()

    tiles = npts // block
    advance(4, 3, 2, 1)
    send_x(3)
    near_part(rown, w, None, 0, tiles // 2)
    relay(0, 1)
    points_next(1)

    advance(4, 3, 2)
    send_x(4)
    near_part(rown, w, None, tiles // 2, tiles)
    relay(2)
    points_next(2)

    advance(4, 3, 2)
    send_x(5)
    for chunk in range(CHUNKS + 1):
        own("own_mate", chunk, 2, mate).wait_recv()
    near_slot(2)
    relay(3)
    relay_on(0, 1)
    points_next(3)

    advance(4, 3, 2)
    send_x(6)
    advance(1, 0)
    couple(0)
    relay(4)
    relay_on(2)
    points_next(4)

    advance(4, 3, 2)
    send_x(7)
    advance(1)
    couple(1)
    relay(5)
    relay_on(3)

    advance(4, 3)
    send_x(8)
    couple(2)
    relay(6)
    relay_on(4)

    advance(4, 3)
    couple(3)
    relay(7)
    relay_on(5)

    advance(4)
    relay(8)
    near_slot(0)
    relay_on(6)

    advance(4)
    couple(4)
    relay_on(7, 8)

    @pl.when(has_behind)
    def _():
        near_slot(1)

    @pl.when(has_behind | jnp.logical_not(direct))
    def _():
        for chunk in range(CHUNKS + 1):
            pass_on("fwd_mate", chunk, 0, 3, mate).wait_recv()
        near_slot(3)

    total = far[...].astype(BF16)

    @pl.loop(0, npts // block)
    def _(at):
        rows = pl.ds(pl.multiple_of(at * block, block), block)
        out[rows] = (near[rows] + dot(interp[rows], total)).astype(out.dtype)

    for chunk in range(CHUNKS + 1):
        own("own_mate", chunk, 2, mate).wait_send()
        own("own_x", chunk, 0, xmate).wait_send()

        @pl.when(has_ahead)
        def _():
            pass_on("fwd", chunk, 0, 1, ahead).wait_send()

        @pl.when(has_behind | direct)
        def _():
            pass_on("fwd_mate", chunk, 0, 3, mate).wait_send()


def per_device(points, weights, interp, transfers, near_mask, skel_index):
    count = lax.axis_size("leaf")
    dim, npts = points.shape
    rhs, rank = weights.shape[1], interp.shape[1]
    levels = transfers.shape[1]
    deep = -(-(dim + 3) // 16) * 16
    slots = plan(levels)
    vmem = pl.BlockSpec(memory_space=pltpu.VMEM)
    return pl.pallas_call(
        functools.partial(body, count, slots),
        out_shape=jax.ShapeDtypeStruct((npts, rhs), BF16),
        in_specs=[vmem] * 4 + [pl.BlockSpec(memory_space=pltpu.SMEM), vmem],
        out_specs=vmem,
        scratch_shapes=[
            pltpu.VMEM((deep, npts), BF16),
            pltpu.VMEM((npts, LANES), BF16),
            pltpu.VMEM((npts, 1), F32),
            pltpu.VMEM((4, deep, npts), BF16),
            pltpu.VMEM((4, npts, rhs), BF16),
            pltpu.VMEM((npts, rhs), F32),
            pltpu.VMEM((rank, rhs), BF16),
            pltpu.VMEM((levels, rank // 2, rhs), F32),
            pltpu.VMEM((levels, rank, rhs), BF16),
            pltpu.VMEM((levels, rank, rhs), BF16),
            pltpu.VMEM((levels, rank, rhs), BF16),
            pltpu.VMEM((levels, rank, LANES), BF16),
            pltpu.VMEM((levels, rank, LANES), BF16),
            pltpu.VMEM((rank, rhs), F32),
            pltpu.SemaphoreType.DMA((len(slots),)),
            pltpu.SemaphoreType.DMA((len(slots),)),
        ],
        compiler_params=pltpu.CompilerParams(
            collective_id=0, has_side_effects=True, vmem_limit_bytes=60 * 2**20
        ),
    )(points, weights, interp, transfers[0], near_mask, skel_index)


def solution(mesh):
    return jax.shard_map(
        per_device,
        mesh=mesh,
        in_specs=(
            P(None, "leaf"),
            P("leaf", None),
            P("leaf", None),
            P("leaf", None, None, None),
            P("leaf", None),
            P("leaf", None),
        ),
        out_specs=P("leaf", None),
        check_vma=False,
    )
```
